32 devices in a mesh: fsdp: 4 (over y, x), ctx: 4 (over z), tp: 2 (over core).
Axes of the slice: x: 2, y: 2, z: 4, core: 2. Of those that a mesh axis runs over, the one named last changes fastest.
Arguments:
- tokens: bfloat16 [16384, 1152], P(('fsdp', 'ctx')), may hold values from -6 to 6
- positions: int32 [16384], P(('fsdp', 'ctx')), may hold values from 0 to 4095, as said below
- query_weight: bfloat16 [1152, 1024], P('fsdp', 'tp'), may hold values from -0.1875 to 0.1875
- keyvalue_weight: bfloat16 [1152, 512], P('fsdp'), may hold values from -0.1875 to 0.1875
- output_weight: bfloat16 [1024, 1152], P('tp', 'fsdp'), may hold values from -0.1875 to 0.1875
- gate_weight: bfloat16 [1152, 6912], P('fsdp', 'tp'), may hold values from -0.1875 to 0.1875
- up_weight: bfloat16 [1152, 6912], P('fsdp', 'tp'), may hold values from -0.1875 to 0.1875
- down_weight: bfloat16 [6912, 1152], P('tp', 'fsdp'), may hold values from -0.078125 to 0.078125
- input_gain: bfloat16 [1152], P('fsdp'), may hold values from -0.5 to 0.5
- query_gain: bfloat16 [256], P('fsdp'), may hold values from -0.5 to 0.5
- key_gain: bfloat16 [256], P('fsdp'), may hold values from -0.5 to 0.5
- attention_gain: bfloat16 [1152], P('fsdp'), may hold values from -0.5 to 0.5
- middle_gain: bfloat16 [1152], P('fsdp'), may hold values from -0.5 to 0.5
- final_gain: bfloat16 [1152], P('fsdp'), may hold values from -0.5 to 0.5
- cotangent: bfloat16 [16384, 1152], P(('fsdp', 'ctx')), may hold values from -6 to 6
Outputs:
- layer_out: bfloat16 [16384, 1152], P(('fsdp', 'ctx'))
- tokens_grad: bfloat16 [16384, 1152], P(('fsdp', 'ctx'))
- query_weight_grad: float32 [1152, 1024], P('fsdp', 'tp')
- keyvalue_weight_grad: float32 [1152, 512], P('fsdp')
- output_weight_grad: float32 [1024, 1152], P('tp', 'fsdp')
- gate_weight_grad: float32 [1152, 6912], P('fsdp', 'tp')
- up_weight_grad: float32 [1152, 6912], P('fsdp', 'tp')
- down_weight_grad: float32 [6912, 1152], P('tp', 'fsdp')
- input_gain_grad: float32 [1152], P('fsdp')
- query_gain_grad: float32 [256], P('fsdp')
- key_gain_grad: float32 [256], P('fsdp')
- attention_gain_grad: float32 [1152], P('fsdp')
- middle_gain_grad: float32 [1152], P('fsdp')
- final_gain_grad: float32 [1152], P('fsdp')
The draws below stay inside these ranges and needn't reach their ends.
Inputs may be any that keep to these rules, and one draw needn't show every extreme that they name: Each run of 4096 tokens of one fsdp index holds whole sequences; within a sequence positions run 0, 1, 2 and so on; every sequence has 1024 tokens or more; some such run holds one sequence only.
All inputs are finite; a program needn't handle non-finite values.
Results may differ from the reference program's by a relative error of at most 0.023.
Values may be sent and summed in bfloat16 or wider, within the bound.
No kernel may reach another device: no remote copies, remote signals or barrier semaphores. Data moves between devices by JAX's collectives and lax.ppermute only.
A program may use at most 256 MiB of HBM per device.

```python
import jax
import jax.numpy as jnp
from jax import lax

D = 1152
HQ = 4
HD = 256
FF = 6912
WINDOW = 512
TOK_DEV = 1024
MIN_LEN = 1024
PACK = 4096
TOKENS = 16384


def draw_positions(key, part):
    unit_count = PACK // MIN_LEN
    pack_count = TOKENS // PACK
    offsets = jax.random.randint(jax.random.fold_in(key, 11), (pack_count, 1), 0, MIN_LEN)
    cut_flags = jax.random.randint(jax.random.fold_in(key, 12), (pack_count, unit_count - 2), 0, 2)
    single_pack = jax.random.randint(jax.random.fold_in(key, 13), (1, 1), 0, pack_count)
    pack_ids = lax.broadcasted_iota(jnp.int32, (pack_count, 1), 0)
    cut_flags = jnp.where(pack_ids == single_pack, 0, cut_flags)
    inside = jnp.arange(PACK, dtype=jnp.int32)
    unit_marks = jnp.arange(1, unit_count - 1, dtype=jnp.int32) * MIN_LEN
    cut_starts = unit_marks[None, :] + offsets
    passed = (inside[None, :, None] >= cut_starts[:, None, :]) & (cut_flags[:, None, :] == 1)
    latest = jnp.max(jnp.where(passed, cut_starts[:, None, :], 0), axis=2)
    return (inside[None, :] - latest).reshape(TOKENS).astype(jnp.int32)


def steps_of(rng, shape, pieces, least, high):
    level, own = 1.0, jax.random.fold_in(rng, 6)
    for axis_at, parts in pieces:
        steps = jnp.exp(jax.random.uniform(jax.random.fold_in(own, axis_at), (parts,), jnp.float32, least / len(pieces), high / len(pieces)))
        level = level * jnp.repeat(steps, shape[axis_at] // parts).reshape([-1 if axis == axis_at else 1 for axis in range(len(shape))])
    return level


def noise(key, shape, spread, most, pieces=(), held_as=jnp.bfloat16):
    array = spread * jax.random.normal(key, shape, jnp.float32)
    if pieces:
        array = array * steps_of(key, shape, pieces, -0.22, 0.18)
    return jnp.clip(array, -most, most).astype(held_as)


def setup_inputs(seed: int = 0) -> dict:
    key_list = jax.random.split(jax.random.key(seed), 16)
    return {
        "tokens": noise(key_list[0], (TOKENS, D), 1.0, 6.0, ((0, 16),)),
        "positions": draw_positions(jax.random.fold_in(key_list[15], 71), 0),
        "query_weight": noise(key_list[2], (D, HQ * HD), D ** -0.5, 0.1875, ((0, 4), (1, 2))),
        "keyvalue_weight": noise(key_list[3], (D, 2 * HD), D ** -0.5, 0.1875, ((0, 4),)),
        "output_weight": noise(key_list[4], (HQ * HD, D), (HQ * HD) ** -0.5, 0.1875, ((0, 2), (1, 4))),
        "gate_weight": noise(key_list[5], (D, FF), D ** -0.5, 0.1875, ((0, 4), (1, 2))),
        "up_weight": noise(key_list[6], (D, FF), D ** -0.5, 0.1875, ((0, 4), (1, 2))),
        "down_weight": noise(key_list[7], (FF, D), FF ** -0.5, 0.078125, ((0, 2), (1, 4))),
        "input_gain": jnp.clip(jax.random.uniform(key_list[8], (D,), jnp.float32, -0.5, 0.5) * steps_of(key_list[8], (D,), ((0, 4),), -0.4, 0.0), -0.5, 0.5).astype(jnp.bfloat16),
        "query_gain": jnp.clip(jax.random.uniform(key_list[9], (HD,), jnp.float32, -0.5, 0.5) * steps_of(key_list[9], (HD,), ((0, 4),), -0.4, 0.0), -0.5, 0.5).astype(jnp.bfloat16),
        "key_gain": jnp.clip(jax.random.uniform(key_list[10], (HD,), jnp.float32, -0.5, 0.5) * steps_of(key_list[10], (HD,), ((0, 4),), -0.4, 0.0), -0.5, 0.5).astype(jnp.bfloat16),
        "attention_gain": jnp.clip(jax.random.uniform(key_list[11], (D,), jnp.float32, -0.5, 0.5) * steps_of(key_list[11], (D,), ((0, 4),), -0.4, 0.0), -0.5, 0.5).astype(jnp.bfloat16),
        "middle_gain": jnp.clip(jax.random.uniform(key_list[12], (D,), jnp.float32, -0.5, 0.5) * steps_of(key_list[12], (D,), ((0, 4),), -0.4, 0.0), -0.5, 0.5).astype(jnp.bfloat16),
        "final_gain": jnp.clip(jax.random.uniform(key_list[13], (D,), jnp.float32, -0.5, 0.5) * steps_of(key_list[13], (D,), ((0, 4),), -0.4, 0.0), -0.5, 0.5).astype(jnp.bfloat16),
        "cotangent": noise(key_list[14], (TOKENS, D), 1.0, 6.0, ((0, 16),)),
    }


EPS = 1e-06
SCALE = 0.0625
NEG = -1e+30
HIGH = lax.Precision.HIGHEST

@jax.custom_vjp
def low(v):
    return lax.optimization_barrier(v.astype(jnp.bfloat16)).astype(jnp.float32)

@jax.custom_vjp
def low_back(v):
    return v

def low_keep(v):
    return (low(v), None)

def low_pass(kept, grad):
    return (grad,)

def back_keep(v):
    return (v, None)

def back_low(kept, grad):
    return (low(grad),)
low.defvjp(low_keep, low_pass)
low_back.defvjp(back_keep, back_low)

def rms_scale(values, gain):
    inverse = lax.rsqrt(lax.optimization_barrier(jnp.mean(values * values, axis=-1, keepdims=True)) + EPS)
    return values * inverse * (1.0 + gain)

def rotate(values, cosine_table, sine_table):
    half_width = values.shape[-1] // 2
    front_half = values[..., :half_width]
    back_half = values[..., half_width:]
    return jnp.concatenate([front_half * cosine_table - back_half * sine_table, back_half * cosine_table + front_half * sine_table], axis=-1)

def rotary(positions):
    half_width = HD // 2
    frequency = 10000.0 ** (-(2.0 * jnp.arange(half_width).astype(jnp.float32)) / HD)
    angles = positions.astype(jnp.float32)[:, None] * frequency[None, :]
    return (jnp.cos(angles), jnp.sin(angles))

def product(left, right):
    return jnp.dot(left, right, precision=HIGH, preferred_element_type=jnp.float32)

def attend(query, key_rows, value_rows, positions):
    block_rows = min(512, TOK_DEV)
    rim_rows = WINDOW - 1
    slab_rows = block_rows + rim_rows
    total_rows = query.shape[0]
    block_count = total_rows // block_rows
    padding = jnp.zeros((rim_rows, HD), jnp.float32)
    key_ext = jnp.concatenate([padding, key_rows], axis=0)
    value_ext = jnp.concatenate([padding, value_rows], axis=0)
    lag_table = jnp.arange(block_rows)[:, None] - jnp.arange(slab_rows)[None, :] + rim_rows
    block_starts = (jnp.arange(block_count) * block_rows).astype(jnp.int32)

    @jax.checkpoint
    def one_block(row_start):
        query_block = lax.dynamic_slice_in_dim(query, row_start, block_rows, 0)
        key_block = lax.dynamic_slice_in_dim(key_ext, row_start, slab_rows, 0)
        value_block = lax.dynamic_slice_in_dim(value_ext, row_start, slab_rows, 0)
        reach = jnp.minimum(lax.dynamic_slice_in_dim(positions, row_start, block_rows, 0), rim_rows)[:, None]
        allowed = (lag_table >= 0) & (lag_table <= reach)
        scores = low_back(jnp.einsum('rhd,sd->hrs', query_block, key_block, precision=HIGH) * SCALE)
        scores = jnp.where(allowed[None], scores, NEG)
        weights = low(jax.nn.softmax(scores, axis=-1))
        return jnp.einsum('hrs,sd->rhd', weights, value_block, precision=HIGH)
    mixed = lax.map(one_block, block_starts)
    return mixed.reshape(total_rows, HQ, HD)

def reference(tokens, positions, query_weight, keyvalue_weight, output_weight, gate_weight, up_weight, down_weight, input_gain, query_gain, key_gain, attention_gain, middle_gain, final_gain, cotangent):
    cosine_table, sine_table = rotary(positions)
    cosine_heads = cosine_table[:, None, :]
    sine_heads = sine_table[:, None, :]

    def layer(inputs, w_query, w_keyvalue, w_output, w_gate, w_up, w_down, g_input, g_query, g_key, g_attention, g_middle, g_final):
        row_count = inputs.shape[0]
        hidden = low(rms_scale(inputs, g_input))
        query_raw = low_back(product(hidden, w_query))
        keyvalue_raw = low_back(product(hidden, w_keyvalue))
        query = query_raw.reshape(row_count, HQ, HD)
        query = low(rotate(rms_scale(query, g_query), cosine_heads, sine_heads))
        key_rows = low(rotate(rms_scale(keyvalue_raw[:, :HD], g_key), cosine_table, sine_table))
        value_rows = low(keyvalue_raw[:, HD:])
        attended = attend(query, key_rows, value_rows, positions).reshape(row_count, HQ * HD)
        attended = low_back(low(attended))
        branch = low_back(product(attended, w_output))
        residual = inputs + rms_scale(branch, g_attention)
        hidden_ffn = low(rms_scale(residual, g_middle))
        gate = low_back(product(hidden_ffn, w_gate))
        upper = low_back(product(hidden_ffn, w_up))
        feed = low(jax.nn.gelu(gate, approximate=True) * upper)
        outcome = low_back(product(feed, w_down))
        return residual + rms_scale(outcome, g_final)
    floats = [arr.astype(jnp.float32) for arr in (tokens, query_weight, keyvalue_weight, output_weight, gate_weight, up_weight, down_weight, input_gain, query_gain, key_gain, attention_gain, middle_gain, final_gain)]
    result, pullback = jax.vjp(layer, *floats)
    grads = pullback(cotangent.astype(jnp.float32))
    return (result.astype(jnp.bfloat16), grads[0].astype(jnp.bfloat16), grads[1], grads[2], grads[3], grads[4], grads[5], grads[6], grads[7], grads[8], grads[9], grads[10], grads[11], grads[12])
```

```python
import jax
import jax.numpy as jnp
from jax import lax
from jax.sharding import PartitionSpec as P


WINDOW = 512
EPS = 1e-06
SCALE = 0.0625
NEG = -1e30
F32 = jnp.float32
BF16 = jnp.bfloat16


def tied(value, *others):
    return lax.optimization_barrier((value,) + others)[0]


def passed_along(value, axis, steps):
    count = lax.axis_size(axis)
    first, last = (max(0, -steps), min(count, count - steps))
    return lax.ppermute(value, axis, [(source, source + steps) for source in range(first, last)])


def hop(value, axis, flip):
    return lax.ppermute(value, axis, [(i, i ^ flip) for i in range(lax.axis_size(axis))])


def summed_tp(part):
    if lax.axis_size("tp") != 2:
        return lax.psum(part, "tp").astype(F32)
    return part.astype(F32) + hop(part, "tp", 1).astype(F32)


def put_rows(full, rows, start):
    return lax.dynamic_update_slice_in_dim(full, rows, start, 0)


def on_square():
    return lax.axis_size("fsdp") == 4


def gather_start(shard):
    if not on_square():
        return (shard,)
    return (shard, hop(shard, "fsdp", 1), hop(shard, "fsdp", 2))


def gather_finish(first):
    shard, near, side = first
    half = shard.shape[0] // 2
    far_top = hop(side[:half], "fsdp", 1)
    far_low = hop(near[half:], "fsdp", 2)
    return (shard, near, side, far_top, far_low)


def placed(pieces, keep):
    shard, near, side, far_top, far_low = pieces
    half = far_top.shape[0]
    me = lax.axis_index("fsdp")
    full = jnp.zeros((4 * keep,) + shard.shape[1:], shard.dtype)
    full = put_rows(full, shard[:keep], me * keep)
    full = put_rows(full, near[:keep], (me ^ 1) * keep)
    full = put_rows(full, side[:keep], (me ^ 2) * keep)
    full = put_rows(full, far_top, (me ^ 3) * keep)
    return put_rows(full, far_low[: keep - half], (me ^ 3) * keep + half)


def assisted():
    return on_square() and lax.axis_size("ctx") % 2 == 0


def wide_start(shard):
    if not assisted():
        return gather_start(shard)
    third = shard.shape[0] // 3
    odd = lax.axis_index("ctx") % 2
    mine = lax.dynamic_slice_in_dim(shard, odd * third, third, 0)
    part = jnp.concatenate([mine, shard[2 * third :]], axis=0)
    return (shard, hop(part, "fsdp", 1), hop(part, "fsdp", 2))


def wide_finish(first):
    if not on_square():
        return lax.all_gather(first[0], "fsdp", axis=0, tiled=True)
    if not assisted():
        return placed(gather_finish(first), first[0].shape[0])
    shard, near, side = first
    rows = shard.shape[0]
    third = rows // 3
    odd = lax.axis_index("ctx") % 2
    me = lax.axis_index("fsdp")
    far_mine = hop(side[:third], "fsdp", 1)
    far_rest = hop(near[third:], "fsdp", 2)
    others = hop(jnp.concatenate([near[:third], side[:third]], axis=0), "ctx", 1)
    far_other = hop(far_mine, "ctx", 1)
    full = jnp.zeros((4 * rows,) + shard.shape[1:], shard.dtype)
    full = put_rows(full, shard, me * rows)
    for flip, mine, other, rest in (
        (1, near[:third], others[:third], near[third:]),
        (2, side[:third], others[third:], side[third:]),
        (3, far_mine, far_other, far_rest),
    ):
        base = (me ^ flip) * rows
        full = put_rows(full, mine, base + odd * third)
        full = put_rows(full, other, base + (1 - odd) * third)
        full = put_rows(full, rest, base + 2 * third)
    return full


def scatter_rows(full, hops):
    if not (hops and on_square()):
        return lax.psum_scatter(full, "fsdp", scatter_dimension=0, tiled=True)
    rows = full.shape[0] // 4
    half = rows // 2
    me = lax.axis_index("fsdp")

    def part(flip, start, size):
        return lax.dynamic_slice_in_dim(full, (me ^ flip) * rows + start, size, 0)

    for_side = hop(part(3, 0, half), "fsdp", 1)
    for_near = hop(part(3, half, rows - half), "fsdp", 2)
    to_near = jnp.concatenate([part(1, 0, half), part(1, half, rows - half) + for_near], axis=0)
    to_side = jnp.concatenate([part(2, 0, half) + for_side, part(2, half, rows - half)], axis=0)
    from_near = hop(to_near, "fsdp", 1)
    from_side = hop(to_side, "fsdp", 2)
    return (
        part(0, 0, rows).astype(F32) + from_near.astype(F32) + from_side.astype(F32)
    ).astype(BF16)


def summed_gains(parts):
    if not (on_square() and lax.axis_size("ctx") == 4):
        whole = lax.psum(parts, ("fsdp", "ctx"))
        return lax.dynamic_index_in_dim(whole, lax.axis_index("fsdp"), 0, keepdims=False)
    me = lax.axis_index("fsdp")

    def part(flip):
        return lax.dynamic_slice_in_dim(parts, me ^ flip, 1, 0)

    mine = part(0)
    for flip in (1, 2, 3):
        mine = mine + hop(part(flip), "fsdp", flip)
    one, two, three = (hop(mine, "ctx", flip) for flip in (1, 2, 3))
    return ((mine + one) + (two + three))[0]


def summed_ctx(share, chunks):
    if chunks == 0 or lax.axis_size("ctx") != 4:
        return lax.psum(share, "ctx")
    here = lax.axis_index("ctx")
    rows = share.shape[0] // chunks
    pieces = []
    for i in range(chunks):
        part = share[i * rows : (i + 1) * rows]
        inward = lax.ppermute(part, "ctx", [(0, 1), (3, 2)])
        pair = part + inward
        across = lax.ppermute(pair, "ctx", [(1, 2), (2, 1)])
        total = pair + across
        outward = lax.ppermute(total, "ctx", [(1, 0), (2, 3)])
        pieces.append(jnp.where((here == 0) | (here == 3), outward, total))
    return jnp.concatenate(pieces, axis=0)


def reduced(full, hops, chunks):
    return summed_ctx(scatter_rows(full, hops), chunks).astype(F32)


def normalize(values):
    inverse = lax.rsqrt(jnp.mean(values * values, axis=-1, keepdims=True) + EPS)
    return (values * inverse, inverse)


def norm_back(gradient, normed, inverse):
    return inverse * (gradient - normed * jnp.mean(gradient * normed, axis=-1, keepdims=True))


def rotate(values, cosine_table, sine_table):
    half_width = values.shape[-1] // 2
    front_half = values[..., :half_width]
    back_half = values[..., half_width:]
    return jnp.concatenate(
        [
            front_half * cosine_table - back_half * sine_table,
            back_half * cosine_table + front_half * sine_table,
        ],
        axis=-1,
    )


def rotary(positions, head_width):
    half_width = head_width // 2
    frequency = 10000.0 ** (-(2.0 * jnp.arange(half_width).astype(F32)) / head_width)
    angles = positions.astype(F32)[:, None] * frequency[None, :]
    return (jnp.cos(angles), jnp.sin(angles))


def product(left, right):
    return jnp.dot(left, right, preferred_element_type=F32)


def inner_rows(left, right):
    return lax.dot_general(left, right, (((0,), (0,)), ((), ())), preferred_element_type=F32)


def inner_cols(left, right):
    return lax.dot_general(left, right, (((1,), (1,)), ((), ())), preferred_element_type=F32)


def layer(
    tokens,
    positions,
    query_weight,
    keyvalue_weight,
    output_weight,
    gate_weight,
    up_weight,
    down_weight,
    input_gain,
    query_gain,
    key_gain,
    attention_gain,
    middle_gain,
    final_gain,
    cotangent,
):
    fsdp = lax.axis_size("fsdp")
    head_width = query_gain.shape[0] * fsdp
    query_width = query_weight.shape[1]
    local_heads = query_width // head_width
    tok_rows = tokens.shape[0]
    block_rows = WINDOW
    block_count = tok_rows // block_rows

    shard_rows = query_weight.shape[0]
    gains = jnp.concatenate(
        [input_gain, attention_gain, middle_gain, final_gain, query_gain, key_gain]
    )
    qkv_shard = jnp.concatenate([query_weight, keyvalue_weight], axis=1)
    output_shard = output_weight.T
    down_shard = down_weight.T
    qkv_first = gather_start(qkv_shard)
    gains = tied(gains[None], qkv_shard)
    if on_square():
        near, side, far = (hop(gains, "fsdp", flip) for flip in (1, 2, 3))
        me = lax.axis_index("fsdp")
        gains_full = jnp.zeros((fsdp, gains.shape[1]), BF16)
        for flip, piece in enumerate((gains, near, side, far)):
            gains_full = put_rows(gains_full, piece, me ^ flip)
        qkv_pieces = gather_finish(qkv_first)
        output_first = gather_start(tied(output_shard, *qkv_pieces[3:]))
        gate_first = wide_start(tied(gate_weight, *qkv_pieces[3:]))
        up_first = wide_start(tied(up_weight, *gate_first[1:]))
        down_first = wide_start(tied(down_shard, *up_first[1:]))
        qkv_full = placed(qkv_pieces, shard_rows)
        output_full = placed(gather_finish(output_first), shard_rows)
    else:
        gains_full = lax.all_gather(gains, "fsdp", axis=0, tiled=True)
        qkv_full = lax.all_gather(qkv_shard, "fsdp", axis=0, tiled=True)
        output_full = lax.all_gather(output_shard, "fsdp", axis=0, tiled=True)
        gate_first, up_first, down_first = (gate_weight,), (up_weight,), (down_shard,)
    gate_full = wide_finish(gate_first)
    up_full = wide_finish(up_first)
    down_full = wide_finish(down_first)
    cuts = [0, shard_rows, 2 * shard_rows, 3 * shard_rows, 4 * shard_rows]
    cuts += [cuts[-1] + query_gain.shape[0], cuts[-1] + query_gain.shape[0] + key_gain.shape[0]]
    factors = [
        1.0 + gains_full[:, low:high].reshape(-1).astype(F32)
        for low, high in zip(cuts[:-1], cuts[1:])
    ]
    input_factor, attention_factor, middle_factor, final_factor, query_factor, key_factor = factors

    inputs = tokens.astype(F32)
    normed_in, inverse_in = normalize(inputs)
    hidden = (normed_in * input_factor).astype(BF16)
    qkv_raw = product(hidden, qkv_full)
    query_raw = qkv_raw[:, :query_width].reshape(tok_rows, local_heads, head_width)
    keyvalue_raw = qkv_raw[:, query_width:]
    cosine_table, sine_table = rotary(positions, head_width)
    cosine_heads = cosine_table[:, None, :]
    sine_heads = sine_table[:, None, :]
    query_normed, query_inverse = normalize(query_raw)
    query_rot = rotate(query_normed * query_factor, cosine_heads, sine_heads).astype(BF16)
    key_normed, key_inverse = normalize(keyvalue_raw[:, :head_width])
    key_rot = rotate(key_normed * key_factor, cosine_table, sine_table)
    keyvalue = jnp.concatenate([key_rot, keyvalue_raw[:, head_width:]], axis=1).astype(BF16)
    earlier = passed_along(keyvalue[tok_rows - WINDOW :], "ctx", 1)

    lag = (
        lax.broadcasted_iota(jnp.int32, (block_rows, 2 * WINDOW), 0)
        - lax.broadcasted_iota(jnp.int32, (block_rows, 2 * WINDOW), 1)
        + WINDOW
    )
    reach = jnp.minimum(positions, WINDOW - 1)[:, None]

    def block_of(index):
        rows = slice(index * block_rows, (index + 1) * block_rows)
        if index == 0:
            slab = jnp.concatenate([earlier, keyvalue[:block_rows]], axis=0)
        else:
            slab = keyvalue[(index - 1) * block_rows : (index + 1) * block_rows]
        query_block = query_rot[rows]
        key_block = slab[:, :head_width]
        value_block = slab[:, head_width:]
        allowed = (lag >= 0) & (lag <= reach[rows])
        scores = (
            jnp.einsum("rhd,sd->hrs", query_block, key_block, preferred_element_type=F32) * SCALE
        )
        return query_block, key_block, value_block, jnp.where(allowed[None], scores, NEG)

    mixed = [None] * block_count
    logsums = [None] * block_count
    for index in reversed(range(block_count)):
        _, _, value_block, scores = block_of(index)
        highest = jnp.max(scores, axis=-1, keepdims=True)
        shifted = jnp.exp(scores - highest)
        totals = jnp.sum(shifted, axis=-1, keepdims=True)
        weights = (shifted / totals).astype(BF16)
        mixed[index] = jnp.einsum(
            "hrs,sd->rhd", weights, value_block, preferred_element_type=F32
        ).astype(BF16)
        logsums[index] = highest + jnp.log(totals)
    attended = jnp.concatenate(mixed, axis=0).reshape(tok_rows, query_width)
    branch = inner_cols(attended, output_full).astype(BF16)
    branch = summed_tp(branch)
    branch_normed, branch_inverse = normalize(branch)
    residual = inputs + branch_normed * attention_factor
    middle_normed, middle_inverse = normalize(residual)
    hidden_ffn = (middle_normed * middle_factor).astype(BF16)

    gate_value = product(hidden_ffn, gate_full)
    up_value = product(hidden_ffn, up_full)
    activated, gelu_pull = jax.vjp(lambda v: jax.nn.gelu(v, approximate=True), gate_value)
    feed = (activated * up_value).astype(BF16)
    outcome = inner_cols(feed, down_full).astype(BF16)
    outcome = summed_tp(outcome)
    outcome_normed, outcome_inverse = normalize(outcome)
    layer_out = (residual + outcome_normed * final_factor).astype(BF16)
    upstream = cotangent.astype(F32)
    final_gain_grad = jnp.sum(upstream * outcome_normed, axis=0)
    outcome_grad = norm_back(upstream * final_factor, outcome_normed, outcome_inverse).astype(BF16)
    down_grad = inner_rows(outcome_grad, feed).astype(BF16)
    outcome_grad = tied(outcome_grad, down_grad)
    feed_grad = product(outcome_grad, down_full)
    gate_grad = gelu_pull(feed_grad * up_value)[0].astype(BF16)
    up_grad = (feed_grad * activated).astype(BF16)
    gate_weight_grad = inner_rows(hidden_ffn, gate_grad).astype(BF16)
    up_grad = tied(up_grad, gate_weight_grad)
    up_weight_grad = inner_rows(hidden_ffn, up_grad).astype(BF16)
    gate_grad, up_grad, _ = lax.optimization_barrier((gate_grad, up_grad, up_weight_grad))
    hidden_part = inner_cols(gate_grad, gate_full)
    hidden_part = (hidden_part + inner_cols(up_grad, up_full)).astype(BF16)
    hidden_ffn_grad = summed_tp(hidden_part)
    middle_gain_grad = jnp.sum(hidden_ffn_grad * middle_normed, axis=0)
    residual_grad = upstream + norm_back(
        hidden_ffn_grad * middle_factor, middle_normed, middle_inverse
    )
    attention_gain_grad = jnp.sum(residual_grad * branch_normed, axis=0)
    branch_grad = norm_back(
        residual_grad * attention_factor, branch_normed, branch_inverse
    ).astype(BF16)
    output_weight_grad = inner_rows(branch_grad, attended).astype(BF16)

    attended_grad = product(branch_grad, output_full).astype(BF16)
    attended_heads = attended_grad.reshape(tok_rows, local_heads, head_width)
    query_parts = [None] * block_count
    slab_grads = [None] * block_count
    for index in range(block_count):
        query_block, key_block, value_block, scores = block_of(index)
        weights = jnp.exp(scores - logsums[index])
        upper_grad = attended_heads[index * block_rows : (index + 1) * block_rows]
        weight_grad = jnp.einsum(
            "rhd,sd->hrs", upper_grad, value_block, preferred_element_type=F32
        )
        centred = jnp.sum(weights * weight_grad, axis=-1, keepdims=True)
        score_grad = (weights * (weight_grad - centred)).astype(BF16)
        query_parts[index] = (
            jnp.einsum("hrs,sd->rhd", score_grad, key_block, preferred_element_type=F32) * SCALE
        )
        key_part = (
            jnp.einsum("hrs,rhd->sd", score_grad, query_block, preferred_element_type=F32) * SCALE
        )
        value_part = jnp.einsum(
            "hrs,rhd->sd", weights.astype(BF16), upper_grad, preferred_element_type=F32
        )
        slab_grads[index] = jnp.concatenate([key_part, value_part], axis=1)
    returned = passed_along(slab_grads[0][:WINDOW].astype(BF16), "ctx", -1)
    own_grads = []
    for index in range(block_count):
        rows = slab_grads[index][WINDOW:]
        if index + 1 < block_count:
            rows = rows + slab_grads[index + 1][:WINDOW]
        else:
            rows = rows + returned.astype(F32)
        own_grads.append(rows)
    keyvalue_grad = summed_tp(jnp.concatenate(own_grads, axis=0).astype(BF16))

    query_turned = jnp.concatenate(query_parts, axis=0)
    query_unturned = rotate(query_turned, cosine_heads, -sine_heads)
    query_gain_part = jnp.sum(query_unturned * query_normed, axis=(0, 1))
    query_raw_grad = (
        norm_back(query_unturned * query_factor, query_normed, query_inverse)
        .reshape(tok_rows, query_width)
        .astype(BF16)
    )
    key_unturned = rotate(keyvalue_grad[:, :head_width], cosine_table, -sine_table)
    key_gain_grad = jnp.sum(key_unturned * key_normed, axis=0)
    key_raw_grad = norm_back(key_unturned * key_factor, key_normed, key_inverse)
    keyvalue_raw_grad = jnp.concatenate(
        [key_raw_grad, keyvalue_grad[:, head_width:]], axis=1
    ).astype(BF16)
    query_part = inner_cols(query_raw_grad, qkv_full[:, :query_width]).astype(BF16)
    qkv_weight_grad = inner_rows(
        hidden, jnp.concatenate([query_raw_grad, keyvalue_raw_grad], axis=1)
    ).astype(BF16)
    hidden_kv = inner_cols(keyvalue_raw_grad, qkv_full[:, query_width:])
    hidden_grad = summed_tp(query_part) + hidden_kv
    input_gain_grad = jnp.sum(hidden_grad * normed_in, axis=0)
    tokens_grad = (
        residual_grad + norm_back(hidden_grad * input_factor, normed_in, inverse_in)
    ).astype(BF16)

    down_share = reduced(down_grad, True, 1).T
    gate_share = reduced(gate_weight_grad, True, 1)
    up_share = reduced(up_weight_grad, False, 3)
    attention_shares = reduced(
        jnp.concatenate([qkv_weight_grad, output_weight_grad], axis=1), True, 1
    )
    query_gain_grad = summed_tp(query_gain_part)
    gain_shares = summed_gains(
        jnp.concatenate(
            [
                grad.reshape(fsdp, -1)
                for grad in (
                    input_gain_grad,
                    attention_gain_grad,
                    middle_gain_grad,
                    final_gain_grad,
                    query_gain_grad,
                    key_gain_grad,
                )
            ],
            axis=1,
        )
    )
    gain_shares = [gain_shares[low:high] for low, high in zip(cuts[:-1], cuts[1:])]
    input_share, attention_share, middle_share, final_share, query_gshare, key_share = gain_shares
    qkv_width = qkv_shard.shape[1]
    qkv_share = attention_shares[:, :qkv_width]
    output_share = attention_shares[:, qkv_width:].T
    return (
        layer_out,
        tokens_grad,
        qkv_share[:, :query_width],
        qkv_share[:, query_width:],
        output_share,
        gate_share,
        up_share,
        down_share,
        input_share,
        query_gshare,
        key_share,
        attention_share,
        middle_share,
        final_share,
    )


def solution(mesh):
    rows = P(("fsdp", "ctx"), None)
    inward = P("fsdp", "tp")
    outward = P("tp", "fsdp")
    gain = P("fsdp")
    whole = P("fsdp", None)
    return jax.shard_map(
        layer,
        mesh=mesh,
        in_specs=(
            (rows, P(("fsdp", "ctx")), inward, whole, outward, inward, inward, outward)
            + (gain,) * 6
            + (rows,)
        ),
        out_specs=(rows, rows, inward, whole, outward, inward, inward, outward) + (gain,) * 6,
        check_vma=False,
    )
```

```python
import jax
import jax.numpy as jnp
from jax import lax
from jax.sharding import PartitionSpec as P


WINDOW = 512
EPS = 1e-06
SCALE = 0.0625
NEG = -1e30
F32 = jnp.float32
BF16 = jnp.bfloat16


def tied(value, *others):
    return lax.optimization_barrier((value,) + others)[0]


def passed_along(value, axis, steps):
    count = lax.axis_size(axis)
    first, last = (max(0, -steps), min(count, count - steps))
    return lax.ppermute(value, axis, [(source, source + steps) for source in range(first, last)])


def hop(value, axis, flip):
    return lax.ppermute(value, axis, [(i, i ^ flip) for i in range(lax.axis_size(axis))])


def summed_tp(part):
    if lax.axis_size("tp") != 2:
        return lax.psum(part, "tp").astype(F32)
    return part.astype(F32) + hop(part, "tp", 1).astype(F32)


def put_rows(full, rows, start):
    return lax.dynamic_update_slice_in_dim(full, rows, start, 0)


def on_square():
    return lax.axis_size("fsdp") == 4


def gather_start(shard):
    if not on_square():
        return (shard,)
    return (shard, hop(shard, "fsdp", 1), hop(shard, "fsdp", 2))


def gather_finish(first):
    shard, near, side = first
    half = shard.shape[0] // 2
    far_top = hop(side[:half], "fsdp", 1)
    far_low = hop(near[half:], "fsdp", 2)
    return (shard, near, side, far_top, far_low)


def placed(pieces, keep):
    shard, near, side, far_top, far_low = pieces
    half = far_top.shape[0]
    me = lax.axis_index("fsdp")
    full = jnp.zeros((4 * keep,) + shard.shape[1:], shard.dtype)
    full = put_rows(full, shard[:keep], me * keep)
    full = put_rows(full, near[:keep], (me ^ 1) * keep)
    full = put_rows(full, side[:keep], (me ^ 2) * keep)
    full = put_rows(full, far_top, (me ^ 3) * keep)
    return put_rows(full, far_low[: keep - half], (me ^ 3) * keep + half)


def assisted():
    return on_square() and lax.axis_size("ctx") % 2 == 0


def wide_start(shard):
    if not assisted():
        return gather_start(shard)
    third = shard.shape[0] // 3
    odd = lax.axis_index("ctx") % 2
    mine = lax.dynamic_slice_in_dim(shard, odd * third, third, 0)
    part = jnp.concatenate([mine, shard[2 * third :]], axis=0)
    return (shard, hop(part, "fsdp", 1), hop(part, "fsdp", 2))


def wide_finish(first):
    if not on_square():
        return lax.all_gather(first[0], "fsdp", axis=0, tiled=True)
    if not assisted():
        return placed(gather_finish(first), first[0].shape[0])
    shard, near, side = first
    rows = shard.shape[0]
    third = rows // 3
    odd = lax.axis_index("ctx") % 2
    me = lax.axis_index("fsdp")
    far_mine = hop(side[:third], "fsdp", 1)
    far_rest = hop(near[third:], "fsdp", 2)
    others = hop(jnp.concatenate([near[:third], side[:third]], axis=0), "ctx", 1)
    far_other = hop(far_mine, "ctx", 1)
    full = jnp.zeros((4 * rows,) + shard.shape[1:], shard.dtype)
    full = put_rows(full, shard, me * rows)
    for flip, mine, other, rest in (
        (1, near[:third], others[:third], near[third:]),
        (2, side[:third], others[third:], side[third:]),
        (3, far_mine, far_other, far_rest),
    ):
        base = (me ^ flip) * rows
        full = put_rows(full, mine, base + odd * third)
        full = put_rows(full, other, base + (1 - odd) * third)
        full = put_rows(full, rest, base + 2 * third)
    return full


def scatter_rows(full, hops):
    if not (hops and on_square()):
        return lax.psum_scatter(full, "fsdp", scatter_dimension=0, tiled=True)
    rows = full.shape[0] // 4
    half = rows // 2
    me = lax.axis_index("fsdp")

    def part(flip, start, size):
        return lax.dynamic_slice_in_dim(full, (me ^ flip) * rows + start, size, 0)

    for_side = hop(part(3, 0, half), "fsdp", 1)
    for_near = hop(part(3, half, rows - half), "fsdp", 2)
    to_near = jnp.concatenate([part(1, 0, half), part(1, half, rows - half) + for_near], axis=0)
    to_side = jnp.concatenate([part(2, 0, half) + for_side, part(2, half, rows - half)], axis=0)
    from_near = hop(to_near, "fsdp", 1)
    from_side = hop(to_side, "fsdp", 2)
    return (
        part(0, 0, rows).astype(F32) + from_near.astype(F32) + from_side.astype(F32)
    ).astype(BF16)


def summed_gains(parts):
    if not (on_square() and lax.axis_size("ctx") == 4):
        whole = lax.psum(parts, ("fsdp", "ctx"))
        return lax.dynamic_index_in_dim(whole, lax.axis_index("fsdp"), 0, keepdims=False)
    me = lax.axis_index("fsdp")

    def part(flip):
        return lax.dynamic_slice_in_dim(parts, me ^ flip, 1, 0)

    mine = part(0)
    near, side, far = (hop(part(flip), "fsdp", flip) for flip in (1, 2, 3))
    mine = ((mine + near) + side) + far
    one, two, three = (hop(mine, "ctx", flip) for flip in (1, 2, 3))
    return ((mine + one) + (two + three))[0]


def summed_ctx(share, chunks):
    if chunks == 0 or lax.axis_size("ctx") != 4:
        return lax.psum(share, "ctx")
    here = lax.axis_index("ctx")
    rows = share.shape[0] // chunks
    pieces = []
    for i in range(chunks):
        part = share[i * rows : (i + 1) * rows]
        inward = lax.ppermute(part, "ctx", [(0, 1), (3, 2)])
        pair = part + inward
        across = lax.ppermute(pair, "ctx", [(1, 2), (2, 1)])
        total = pair + across
        outward = lax.ppermute(total, "ctx", [(1, 0), (2, 3)])
        pieces.append(jnp.where((here == 0) | (here == 3), outward, total))
    return jnp.concatenate(pieces, axis=0)


def reduced(full, hops, chunks):
    return summed_ctx(scatter_rows(full, hops), chunks).astype(F32)


def normalize(values):
    inverse = lax.rsqrt(jnp.mean(values * values, axis=-1, keepdims=True) + EPS)
    return (values * inverse, inverse)


def norm_back(gradient, normed, inverse):
    return inverse * (gradient - normed * jnp.mean(gradient * normed, axis=-1, keepdims=True))


def rotate(values, cosine_table, sine_table):
    half_width = values.shape[-1] // 2
    front_half = values[..., :half_width]
    back_half = values[..., half_width:]
    return jnp.concatenate(
        [
            front_half * cosine_table - back_half * sine_table,
            back_half * cosine_table + front_half * sine_table,
        ],
        axis=-1,
    )


def rotary(positions, head_width):
    half_width = head_width // 2
    frequency = 10000.0 ** (-(2.0 * jnp.arange(half_width).astype(F32)) / head_width)
    angles = positions.astype(F32)[:, None] * frequency[None, :]
    return (jnp.cos(angles), jnp.sin(angles))


def product(left, right):
    return jnp.dot(left, right, preferred_element_type=F32)


def inner_rows(left, right):
    return lax.dot_general(left, right, (((0,), (0,)), ((), ())), preferred_element_type=F32)


def inner_cols(left, right):
    return lax.dot_general(left, right, (((1,), (1,)), ((), ())), preferred_element_type=F32)


def layer(
    tokens,
    positions,
    query_weight,
    keyvalue_weight,
    output_weight,
    gate_weight,
    up_weight,
    down_weight,
    input_gain,
    query_gain,
    key_gain,
    attention_gain,
    middle_gain,
    final_gain,
    cotangent,
):
    fsdp = lax.axis_size("fsdp")
    head_width = query_gain.shape[0] * fsdp
    query_width = query_weight.shape[1]
    local_heads = query_width // head_width
    tok_rows = tokens.shape[0]
    block_rows = WINDOW
    block_count = tok_rows // block_rows

    shard_rows = query_weight.shape[0]
    gains = jnp.concatenate(
        [input_gain, attention_gain, middle_gain, final_gain, query_gain, key_gain]
    )
    qkv_shard = jnp.concatenate([query_weight, keyvalue_weight], axis=1)
    output_shard = output_weight.T
    down_shard = down_weight.T
    qkv_first = gather_start(qkv_shard)
    gains = tied(gains[None], qkv_shard)
    if on_square():
        near, side, far = (hop(gains, "fsdp", flip) for flip in (1, 2, 3))
        me = lax.axis_index("fsdp")
        gains_full = jnp.zeros((fsdp, gains.shape[1]), BF16)
        for flip, piece in enumerate((gains, near, side, far)):
            gains_full = put_rows(gains_full, piece, me ^ flip)
        qkv_pieces = gather_finish(qkv_first)
        output_first = gather_start(tied(output_shard, *qkv_pieces[3:]))
        gate_first = wide_start(tied(gate_weight, *qkv_pieces[3:]))
        up_first = wide_start(tied(up_weight, *gate_first[1:]))
        down_first = wide_start(tied(down_shard, *up_first[1:]))
        qkv_full = placed(qkv_pieces, shard_rows)
        output_full = placed(gather_finish(output_first), shard_rows)
    else:
        gains_full = lax.all_gather(gains, "fsdp", axis=0, tiled=True)
        qkv_full = lax.all_gather(qkv_shard, "fsdp", axis=0, tiled=True)
        output_full = lax.all_gather(output_shard, "fsdp", axis=0, tiled=True)
        gate_first, up_first, down_first = (gate_weight,), (up_weight,), (down_shard,)
    gate_full = wide_finish(gate_first)
    up_full = wide_finish(up_first)
    down_full = wide_finish(down_first)
    cuts = [0, shard_rows, 2 * shard_rows, 3 * shard_rows, 4 * shard_rows]
    cuts += [cuts[-1] + query_gain.shape[0], cuts[-1] + query_gain.shape[0] + key_gain.shape[0]]
    factors = [
        1.0 + gains_full[:, low:high].reshape(-1).astype(F32)
        for low, high in zip(cuts[:-1], cuts[1:])
    ]
    input_factor, attention_factor, middle_factor, final_factor, query_factor, key_factor = factors

    inputs = tokens.astype(F32)
    normed_in, inverse_in = normalize(inputs)
    hidden = (normed_in * input_factor).astype(BF16)
    qkv_raw = product(hidden, qkv_full)
    query_raw = qkv_raw[:, :query_width].reshape(tok_rows, local_heads, head_width)
    keyvalue_raw = qkv_raw[:, query_width:]
    cosine_table, sine_table = rotary(positions, head_width)
    cosine_heads = cosine_table[:, None, :]
    sine_heads = sine_table[:, None, :]
    query_normed, query_inverse = normalize(query_raw)
    query_rot = rotate(query_normed * query_factor, cosine_heads, sine_heads).astype(BF16)
    key_normed, key_inverse = normalize(keyvalue_raw[:, :head_width])
    key_rot = rotate(key_normed * key_factor, cosine_table, sine_table)
    keyvalue = jnp.concatenate([key_rot, keyvalue_raw[:, head_width:]], axis=1).astype(BF16)
    earlier = passed_along(keyvalue[tok_rows - WINDOW :], "ctx", 1)

    lag = (
        lax.broadcasted_iota(jnp.int32, (block_rows, 2 * WINDOW), 0)
        - lax.broadcasted_iota(jnp.int32, (block_rows, 2 * WINDOW), 1)
        + WINDOW
    )
    reach = jnp.minimum(positions, WINDOW - 1)[:, None]

    def block_of(index):
        rows = slice(index * block_rows, (index + 1) * block_rows)
        if index == 0:
            slab = jnp.concatenate([earlier, keyvalue[:block_rows]], axis=0)
        else:
            slab = keyvalue[(index - 1) * block_rows : (index + 1) * block_rows]
        query_block = query_rot[rows]
        key_block = slab[:, :head_width]
        value_block = slab[:, head_width:]
        allowed = (lag >= 0) & (lag <= reach[rows])
        scores = (
            jnp.einsum("rhd,sd->hrs", query_block, key_block, preferred_element_type=F32) * SCALE
        )
        return query_block, key_block, value_block, jnp.where(allowed[None], scores, NEG)

    mixed = [None] * block_count
    logsums = [None] * block_count
    for index in reversed(range(block_count)):
        _, _, value_block, scores = block_of(index)
        highest = jnp.max(scores, axis=-1, keepdims=True)
        shifted = jnp.exp(scores - highest)
        totals = jnp.sum(shifted, axis=-1, keepdims=True)
        weights = (shifted / totals).astype(BF16)
        mixed[index] = jnp.einsum(
            "hrs,sd->rhd", weights, value_block, preferred_element_type=F32
        ).astype(BF16)
        logsums[index] = highest + jnp.log(totals)
    attended = jnp.concatenate(mixed, axis=0).reshape(tok_rows, query_width)
    branch = inner_cols(attended, output_full).astype(BF16)
    branch = summed_tp(branch)
    branch_normed, branch_inverse = normalize(branch)
    residual = inputs + branch_normed * attention_factor
    middle_normed, middle_inverse = normalize(residual)
    hidden_ffn = (middle_normed * middle_factor).astype(BF16)

    gate_value = product(hidden_ffn, gate_full)
    up_value = product(hidden_ffn, up_full)
    activated, gelu_pull = jax.vjp(lambda v: jax.nn.gelu(v, approximate=True), gate_value)
    feed = (activated * up_value).astype(BF16)
    outcome = inner_cols(feed, down_full).astype(BF16)
    outcome = summed_tp(outcome)
    outcome_normed, outcome_inverse = normalize(outcome)
    layer_out = (residual + outcome_normed * final_factor).astype(BF16)
    upstream = cotangent.astype(F32)
    final_gain_grad = jnp.sum(upstream * outcome_normed, axis=0)
    outcome_grad = norm_back(upstream * final_factor, outcome_normed, outcome_inverse).astype(BF16)
    down_grad = inner_rows(outcome_grad, feed).astype(BF16)
    outcome_grad = tied(outcome_grad, down_grad)
    feed_grad = product(outcome_grad, down_full)
    gate_grad = gelu_pull(feed_grad * up_value)[0].astype(BF16)
    up_grad = (feed_grad * activated).astype(BF16)
    gate_weight_grad = inner_rows(hidden_ffn, gate_grad).astype(BF16)
    up_grad = tied(up_grad, gate_weight_grad)
    up_weight_grad = inner_rows(hidden_ffn, up_grad).astype(BF16)
    gate_grad, up_grad, _ = lax.optimization_barrier((gate_grad, up_grad, up_weight_grad))
    hidden_part = inner_cols(gate_grad, gate_full)
    hidden_part = (hidden_part + inner_cols(up_grad, up_full)).astype(BF16)
    hidden_ffn_grad = summed_tp(hidden_part)
    middle_gain_grad = jnp.sum(hidden_ffn_grad * middle_normed, axis=0)
    residual_grad = upstream + norm_back(
        hidden_ffn_grad * middle_factor, middle_normed, middle_inverse
    )
    attention_gain_grad = jnp.sum(residual_grad * branch_normed, axis=0)
    branch_grad = norm_back(
        residual_grad * attention_factor, branch_normed, branch_inverse
    ).astype(BF16)
    output_weight_grad = inner_rows(branch_grad, attended).astype(BF16)

    attended_grad = product(branch_grad, output_full).astype(BF16)
    attended_heads = attended_grad.reshape(tok_rows, local_heads, head_width)
    query_parts = [None] * block_count
    slab_grads = [None] * block_count
    for index in range(block_count):
        query_block, key_block, value_block, scores = block_of(index)
        weights = jnp.exp(scores - logsums[index])
        upper_grad = attended_heads[index * block_rows : (index + 1) * block_rows]
        weight_grad = jnp.einsum("rhd,sd->hrs", upper_grad, value_block, preferred_element_type=F32)
        centred = jnp.sum(weights * weight_grad, axis=-1, keepdims=True)
        score_grad = (weights * (weight_grad - centred)).astype(BF16)
        query_parts[index] = (
            jnp.einsum("hrs,sd->rhd", score_grad, key_block, preferred_element_type=F32) * SCALE
        )
        key_part = (
            jnp.einsum("hrs,rhd->sd", score_grad, query_block, preferred_element_type=F32) * SCALE
        )
        value_part = jnp.einsum(
            "hrs,rhd->sd", weights.astype(BF16), upper_grad, preferred_element_type=F32
        )
        slab_grads[index] = jnp.concatenate([key_part, value_part], axis=1)
    returned = passed_along(slab_grads[0][:WINDOW].astype(BF16), "ctx", -1)
    own_grads = []
    for index in range(block_count):
        rows = slab_grads[index][WINDOW:]
        if index + 1 < block_count:
            rows = rows + slab_grads[index + 1][:WINDOW]
        else:
            rows = rows + returned.astype(F32)
        own_grads.append(rows)
    own_grads = jnp.concatenate(own_grads, axis=0).astype(BF16)
    keyvalue_grad = summed_tp(own_grads)

    query_turned = jnp.concatenate(query_parts, axis=0)
    query_unturned = rotate(query_turned, cosine_heads, -sine_heads)
    query_gain_part = jnp.sum(query_unturned * query_normed, axis=(0, 1))
    query_raw_grad = (
        norm_back(query_unturned * query_factor, query_normed, query_inverse)
        .reshape(tok_rows, query_width)
        .astype(BF16)
    )
    key_unturned = rotate(keyvalue_grad[:, :head_width], cosine_table, -sine_table)
    key_gain_grad = jnp.sum(key_unturned * key_normed, axis=0)
    key_raw_grad = norm_back(key_unturned * key_factor, key_normed, key_inverse)
    keyvalue_raw_grad = jnp.concatenate(
        [key_raw_grad, keyvalue_grad[:, head_width:]], axis=1
    ).astype(BF16)
    query_part = inner_cols(query_raw_grad, qkv_full[:, :query_width]).astype(BF16)
    qkv_weight_grad = inner_rows(
        hidden, jnp.concatenate([query_raw_grad, keyvalue_raw_grad], axis=1)
    ).astype(BF16)
    hidden_kv = inner_cols(keyvalue_raw_grad, qkv_full[:, query_width:])
    hidden_grad = summed_tp(query_part) + hidden_kv
    input_gain_grad = jnp.sum(hidden_grad * normed_in, axis=0)
    tokens_grad = (
        residual_grad + norm_back(hidden_grad * input_factor, normed_in, inverse_in)
    ).astype(BF16)

    down_share = reduced(down_grad, True, 2).T
    gate_share = reduced(gate_weight_grad, False, 1)
    attention_part = scatter_rows(
        jnp.concatenate([qkv_weight_grad, output_weight_grad], axis=1), True
    )
    attention_shares = summed_ctx(attention_part, 1).astype(F32)
    up_share = tied(scatter_rows(up_weight_grad, False), attention_part)
    up_share = summed_ctx(up_share, 3).astype(F32)
    query_gain_grad = summed_tp(query_gain_part)
    gain_shares = summed_gains(
        jnp.concatenate(
            [
                grad.reshape(fsdp, -1)
                for grad in (
                    input_gain_grad,
                    attention_gain_grad,
                    middle_gain_grad,
                    final_gain_grad,
                    query_gain_grad,
                    key_gain_grad,
                )
            ],
            axis=1,
        )
    )
    gain_shares = [gain_shares[low:high] for low, high in zip(cuts[:-1], cuts[1:])]
    input_share, attention_share, middle_share, final_share, query_gshare, key_share = gain_shares
    qkv_width = qkv_shard.shape[1]
    qkv_share = attention_shares[:, :qkv_width]
    output_share = attention_shares[:, qkv_width:].T
    return (
        layer_out,
        tokens_grad,
        qkv_share[:, :query_width],
        qkv_share[:, query_width:],
        output_share,
        gate_share,
        up_share,
        down_share,
        input_share,
        query_gshare,
        key_share,
        attention_share,
        middle_share,
        final_share,
    )


def solution(mesh):
    rows = P(("fsdp", "ctx"), None)
    inward = P("fsdp", "tp")
    outward = P("tp", "fsdp")
    gain = P("fsdp")
    whole = P("fsdp", None)
    return jax.shard_map(
        layer,
        mesh=mesh,
        in_specs=(
            (rows, P(("fsdp", "ctx")), inward, whole, outward, inward, inward, outward)
            + (gain,) * 6
            + (rows,)
        ),
        out_specs=(rows, rows, inward, whole, outward, inward, inward, outward) + (gain,) * 6,
        check_vma=False,
    )
```
